32 devices in a mesh: dp: 16 (over z, x, core), mp: 2 (over y).
Axes of the slice: x: 2, y: 2, z: 4, core: 2. Of those that a mesh axis runs over, the one named last changes fastest.
Arguments:
- tokens: bfloat16 [16384, 1024], P('dp'), may hold values from -60 to 60
- w_query: bfloat16 [1024, 1024], P('dp', 'mp'), may hold values from -0.25 to 0.25
- w_key: bfloat16 [1024, 1024], P('dp', 'mp'), may hold values from -0.25 to 0.25
- w_value: bfloat16 [1024, 1024], P('dp', 'mp'), may hold values from -0.1875 to 0.1875
- w_out: bfloat16 [1024, 1024], P('mp', 'dp'), may hold values from -0.5 to 0.5
- w_gate: bfloat16 [1024, 2816], P('dp', 'mp'), may hold values from -0.1875 to 0.1875
- w_up: bfloat16 [1024, 2816], P('dp', 'mp'), may hold values from -0.1875 to 0.1875
- w_down: bfloat16 [2816, 1024], P('mp', 'dp'), may hold values from -0.109375 to 0.109375
- out_grad: bfloat16 [16384, 1024], P('dp'), may hold values from -6 to 6
Outputs:
- block_out: bfloat16 [16384, 1024], P('dp')
- grad_tokens: bfloat16 [16384, 1024], P('dp')
- grad_query: float32 [1024, 1024], P('dp', 'mp')
- grad_key: float32 [1024, 1024], P('dp', 'mp')
- grad_value: float32 [1024, 1024], P('dp', 'mp')
- grad_out: float32 [1024, 1024], P('mp', 'dp')
- grad_gate: float32 [1024, 2816], P('dp', 'mp')
- grad_up: float32 [1024, 2816], P('dp', 'mp')
- grad_down: float32 [2816, 1024], P('mp', 'dp')
The draws below stay inside these ranges and needn't reach their ends.
All inputs are finite; a program needn't handle non-finite values.
Results may differ from the reference program's by a relative error of at most 0.014.
Values may be sent and summed in bfloat16 or wider, within the bound.
A program may use at most 128 MiB of HBM per device.

```python
import math
import jax
import jax.numpy as jnp
from jax import lax

D = 1024
HEADS = 16
FF = 2816
BLK = 64
TOKENS = 16384


def draw_tokens(key, part):
    base_key = jax.random.fold_in(key, 7)
    row_key, column_key, main_key = jax.random.split(base_key, 3)
    low_end = math.log(0.3)
    high_end = math.log(3.0)
    row_scale = jnp.exp(jax.random.uniform(row_key, (TOKENS, 1), jnp.float32, low_end, high_end))
    column_scale = jnp.exp(jax.random.uniform(column_key, (1, D), jnp.float32, low_end, high_end))
    main = jnp.clip(jax.random.normal(main_key, (TOKENS, D), jnp.float32), -6.0, 6.0)
    return (main * row_scale * column_scale).astype(jnp.bfloat16)


def with_spikes(drawn, key, source, target, blocks, factor):
    owner, partner = [(jnp.arange(drawn.shape[axis_at]) // (drawn.shape[axis_at] // blocks)).reshape([-1 if axis == axis_at else 1 for axis in range(drawn.ndim)]) for axis_at in (source, target)]
    chosen = jax.random.permutation(key, blocks)[partner]
    strong = (owner == chosen) | (owner == (partner + blocks // 2) % blocks)
    return jnp.where(strong, factor * drawn, drawn)


def levels(rng, shape, pieces, smallest, largest):
    level, own = 1.0, jax.random.fold_in(rng, 6)
    for position, parts in pieces:
        draws = jnp.exp(jax.random.uniform(jax.random.fold_in(own, position), (parts,), jnp.float32, smallest / len(pieces), largest / len(pieces)))
        level = level * jnp.repeat(draws, shape[position] // parts).reshape([-1 if axis == position else 1 for axis in range(len(shape))])
    return level


def bell_draw(stream_key, extent, deviation, most, cuts=(), kind=jnp.bfloat16):
    drawn = deviation * jax.random.normal(stream_key, extent, jnp.float32)
    if cuts:
        drawn = drawn * levels(stream_key, extent, cuts, -0.22, 0.18)
    return jnp.clip(drawn, -most, most).astype(kind)


def bell_draw_with(own_key, shape, scale, most, pieces, heavy, kind=jnp.bfloat16):
    result = scale * jax.random.normal(own_key, shape, jnp.float32)
    if pieces:
        result = result * levels(own_key, shape, pieces, -0.22, 0.18)
    return jnp.clip(with_spikes(result, jax.random.fold_in(own_key, 3), *heavy), -most, most).astype(kind)


def setup_inputs(seed: int = 0) -> dict:
    splits = jax.random.split(jax.random.key(seed), 10)
    tokens = draw_tokens(jax.random.fold_in(splits[9], 71), 0)
    w_query = bell_draw(splits[1], (D, D), (D // 2) ** -0.5, 0.25, ((0, 16), (1, 2)))
    w_key = bell_draw(splits[2], (D, D), (D // 2) ** -0.5, 0.25, ((0, 16), (1, 2)))
    w_value = bell_draw(splits[3], (D, D), D ** -0.5, 0.1875, ((0, 16), (1, 2)))
    w_out = bell_draw(splits[4], (D, D), (D // 8) ** -0.5, 0.5, ((0, 2), (1, 16)))
    w_gate = bell_draw(splits[5], (D, FF), D ** -0.5, 0.1875, ((0, 16), (1, 2)))
    w_up = bell_draw(splits[6], (D, FF), D ** -0.5, 0.1875, ((0, 16), (1, 2)))
    w_down = bell_draw(splits[7], (FF, D), FF ** -0.5, 0.109375, ((0, 2), (1, 16)))
    out_grad = bell_draw_with(splits[8], (TOKENS, D), 1.0, 6.0, ((0, 16),), (0, 1, 16, 2.0))
    return {"tokens": tokens, "w_query": w_query, "w_key": w_key, "w_value": w_value, "w_out": w_out, "w_gate": w_gate, "w_up": w_up, "w_down": w_down, "out_grad": out_grad}


eps = 1e-06

@jax.custom_vjp
def low(v):
    return lax.optimization_barrier(v.astype(jnp.bfloat16)).astype(jnp.float32)

@jax.custom_vjp
def low_back(v):
    return v

def low_keep(v):
    return (low(v), None)

def low_pass(kept, grad):
    return (grad,)

def back_keep(v):
    return (v, None)

def back_low(kept, grad):
    return (low(grad),)
low.defvjp(low_keep, low_pass)
low_back.defvjp(back_keep, back_low)

def normalize(values_in):
    return values_in * lax.rsqrt(lax.optimization_barrier(jnp.mean(values_in * values_in, axis=-1, keepdims=True)) + eps)

def product(left, right):
    return jnp.dot(left, right, precision=lax.Precision.HIGHEST, preferred_element_type=jnp.float32)

def layer(tokens_f, w_query, w_key, w_value, w_out, w_gate, w_up, w_down):
    count = tokens_f.shape[0]
    blocks = count // BLK
    head_dim = D // HEADS
    scale = head_dim ** (-0.5)
    places = jnp.arange(BLK)
    causal = places[:, None] >= places[None, :]

    def split_heads(matrix):
        return matrix.reshape(blocks, BLK, HEADS, head_dim).transpose(0, 2, 1, 3)
    input_one = low(normalize(tokens_f))
    query = split_heads(low_back(low(product(input_one, w_query))))
    keys = split_heads(low_back(low(product(input_one, w_key))))
    values = split_heads(low_back(low(product(input_one, w_value))))
    raw = scale * jnp.einsum('bhqd,bhkd->bhqk', query, keys, precision=lax.Precision.HIGHEST)
    scores = low_back(jnp.where(causal, raw, -1e+30))
    attend = jax.nn.softmax(scores, axis=-1)
    mixed = jnp.einsum('bhqk,bhkd->bhqd', low(attend), values, precision=lax.Precision.HIGHEST)
    mixed = low_back(low(mixed.transpose(0, 2, 1, 3).reshape(count, D)))
    branch_one = low_back(product(mixed, w_out))
    resid = tokens_f + branch_one
    input_two = low(normalize(resid))
    gate = low_back(product(input_two, w_gate))
    upper = low_back(product(input_two, w_up))
    hidden = low(gate * upper)
    return resid + product(hidden, w_down)

def reference(tokens, w_query, w_key, w_value, w_out, w_gate, w_up, w_down, out_grad):
    weights = tuple((matrix.astype(jnp.float32) for matrix in (w_query, w_key, w_value, w_out, w_gate, w_up, w_down)))
    group = math.gcd(TOKENS, 2048)
    groups = TOKENS // group
    tokens_all = tokens.astype(jnp.float32).reshape(groups, group, D)
    grads_all = out_grad.astype(jnp.float32).reshape(groups, group, D)

    def advance(carry, item):
        tokens_group, grad_group = item
        outcome, pull = jax.vjp(layer, tokens_group, *weights)
        pulled = pull(grad_group)
        carry = tuple((total + piece for total, piece in zip(carry, pulled[1:])))
        return (carry, (outcome.astype(jnp.bfloat16), pulled[0].astype(jnp.bfloat16)))
    start = tuple((jnp.zeros(matrix.shape, jnp.float32) for matrix in weights))
    totals, (outs_all, backs_all) = lax.scan(advance, start, (tokens_all, grads_all))
    return (outs_all.reshape(TOKENS, D), backs_all.reshape(TOKENS, D), totals[0], totals[1], totals[2], totals[3], totals[4], totals[5], totals[6])
```

```python
import functools

import jax
import jax.numpy as jnp
from jax import lax
from jax.experimental import pallas as pl
from jax.experimental.pallas import tpu as pltpu
from jax.sharding import PartitionSpec as P

HEADS = 16
BLK = 64
MICRO = 2

eps = 1e-06

F32 = jnp.float32
BF16 = jnp.bfloat16
MESH = pl.DeviceIdType.MESH
NZ = 4
HALF = 128
WIDE = 256
ATT_CHUNKS = 4
ROWS = 64


def dot_nn(left, right):
    return lax.dot_general(left, right, (((1,), (0,)), ((), ())), preferred_element_type=F32)


def dot_nt(left, right):
    return lax.dot_general(left, right, (((1,), (1,)), ((), ())), preferred_element_type=F32)


def dot_tn(left, right):
    return lax.dot_general(left, right, (((0,), (0,)), ((), ())), preferred_element_type=F32)


def row_factor(values):
    return lax.rsqrt(jnp.mean(values * values, axis=-1, keepdims=True) + eps)


def layer_kernel(
    ff_chunks, ff_width,
    tok_hbm, og_hbm, ash, ssh,
    bo_hbm, gt_hbm, ga_hbm, gs_hbm,
    wa, ws, tok, in1, qb, kb, vb, mixed, att, resid, in2, in2t, og, ogt, n2b, b2, hgu,
    nland, bland, l0s, l1s, l2s, l0a, l1a, l2a, l3a, gout_a, gout_s,
    loc_sem, a_s, a_r, b_s, b_r, r_s, r_r, q_s, q_r, y_s, y_r, out_sem, credit_s, credit_a,
):
    dp = lax.axis_index("dp")
    y = lax.axis_index("mp")
    z = lax.div(dp, 4)
    x = lax.rem(lax.div(dp, 2), 2)
    c = lax.rem(dp, 2)
    ox, oy, oc = 1 - x, 1 - y, 1 - c

    def at_dev(zz, xx, cc, yy):
        return (zz * 4 + xx * 2 + cc, yy)

    dev_x = at_dev(z, ox, c, y)
    dev_y = at_dev(z, x, c, oy)
    dev_c = at_dev(z, x, oc, y)
    z_to = [lax.rem(z + k, NZ) for k in (1, 2, 3)]
    z_from = [lax.rem(z + NZ - k, NZ) for k in (1, 2, 3)]
    dev_z = [at_dev(t, x, c, y) for t in z_to]

    def remote(src, dst, ssem, rsem, device):
        return pltpu.make_async_remote_copy(
            src_ref=src, dst_ref=dst, send_sem=ssem, recv_sem=rsem,
            device_id=device, device_id_type=MESH,
        )

    def send(src, dst, ssem, rsem, device):
        remote(src, dst, ssem, rsem, device).start()

    def got(dst, ssem, rsem):
        remote(dst, dst, ssem, rsem, dev_c).wait_recv()

    def sent(src, ssem, rsem):
        remote(src, src, ssem, rsem, dev_c).wait_send()

    barrier = pltpu.get_barrier_semaphore()
    for device in [dev_c, dev_x, dev_y] + dev_z:
        pl.semaphore_signal(barrier, inc=1, device_id=device, device_id_type=MESH)

    own = y * 512
    peer = oy * 512
    in_tok = pltpu.make_async_copy(tok_hbm.at[pl.ds(own, 512)], tok, loc_sem.at[0])
    in_og = pltpu.make_async_copy(og_hbm, og, loc_sem.at[1])
    in_tok.start()
    in_og.start()
    pl.semaphore_wait(barrier, 6)

    ycol = pl.ds(y * HALF, HALF)
    oycol = pl.ds(oy * HALF, HALF)

    def a_slot(h, zz, xx, cc, col):
        return wa.at[h, :, zz, xx, cc, :, col]

    allz = slice(None)

    def A1(h):
        for k in range(3):
            send(ash.at[h], a_slot(h, z, x, c, ycol), a_s.at[h, k], a_r.at[h, k], dev_z[k])
        pltpu.make_async_copy(ash.at[h], a_slot(h, z, x, c, ycol), loc_sem.at[2 + h]).start()

    def A2(h):
        for k in range(3):
            got(a_slot(h, z_from[k], x, c, ycol), a_s.at[h, k], a_r.at[h, k])
        pltpu.make_async_copy(ash.at[h], a_slot(h, z, x, c, ycol), loc_sem.at[2 + h]).wait()
        mine = a_slot(h, allz, x, c, ycol)
        first, second = (dev_x, dev_y) if h % 2 == 0 else (dev_y, dev_x)
        send(mine, mine, a_s.at[h, 3], a_r.at[h, 3], first)
        send(mine, mine, a_s.at[h, 4], a_r.at[h, 4], second)
        send(mine, mine, a_s.at[h, 6], a_r.at[h, 6], dev_c)

    def a_from_x(h):
        return a_slot(h, allz, ox, c, ycol)

    def a_from_y(h):
        return a_slot(h, allz, x, c, oycol)

    def a_first(h):
        return a_from_x(h) if h % 2 == 0 else a_from_y(h)

    def a_second(h):
        return a_from_y(h) if h % 2 == 0 else a_from_x(h)

    def a_corner(h):
        return a_slot(h, allz, ox, c, oycol)

    def A3(h):
        got(a_first(h), a_s.at[h, 3], a_r.at[h, 3])
        second = dev_y if h % 2 == 0 else dev_x
        part = a_first(h)
        send(part, part, a_s.at[h, 5], a_r.at[h, 5], second)
        send(part, part, a_s.at[h, 7], a_r.at[h, 7], dev_c)

    def A4(h):
        got(a_second(h), a_s.at[h, 4], a_r.at[h, 4])
        part = a_second(h)
        send(part, part, a_s.at[h, 8], a_r.at[h, 8], dev_c)
        got(a_corner(h), a_s.at[h, 5], a_r.at[h, 5])
        part = a_corner(h)
        send(part, part, a_s.at[h, 9], a_r.at[h, 9], dev_c)

    def A5(h):
        part = a_slot(h, allz, x, oc, ycol)
        for k in range(6, 10):
            got(part, a_s.at[h, k], a_r.at[h, k])

    def a_sent(h):
        for k in range(3):
            sent(ash.at[h], a_s.at[h, k], a_r.at[h, k])
        mine = a_slot(h, allz, x, c, ycol)
        for k in range(3, 10):
            sent(mine, a_s.at[h, k], a_r.at[h, k])

    def width(j):
        return min(WIDE, ff_width - j * WIDE)

    def b_slot(j, zz, xx, cc):
        return ws.at[j, :, zz, xx, cc, :, pl.ds(0, width(j))]

    def b_shard(j):
        return ssh.at[j, :, :, pl.ds(0, width(j))]

    def B1(j):
        for k in range(3):
            send(b_shard(j), b_slot(j, z, x, c), b_s.at[j, k], b_r.at[j, k], dev_z[k])
        pltpu.make_async_copy(b_shard(j), b_slot(j, z, x, c), loc_sem.at[2 + ATT_CHUNKS + j]).start()

    def B2(j):
        for k in range(3):
            got(b_slot(j, z_from[k], x, c), b_s.at[j, k], b_r.at[j, k])
        pltpu.make_async_copy(b_shard(j), b_slot(j, z, x, c), loc_sem.at[2 + ATT_CHUNKS + j]).wait()
        mine = b_slot(j, allz, x, c)
        send(mine, mine, b_s.at[j, 3], b_r.at[j, 3], dev_x)
        send(mine, mine, b_s.at[j, 4], b_r.at[j, 4], dev_c)

    def B3(j):
        part = b_slot(j, allz, ox, c)
        got(part, b_s.at[j, 3], b_r.at[j, 3])
        send(part, part, b_s.at[j, 5], b_r.at[j, 5], dev_c)

    def B5(j):
        got(b_slot(j, allz, x, oc), b_s.at[j, 4], b_r.at[j, 4])
        got(b_slot(j, allz, ox, oc), b_s.at[j, 5], b_r.at[j, 5])

    def b_sent(j):
        for k in range(3):
            sent(b_shard(j), b_s.at[j, k], b_r.at[j, k])
        for k in range(3, 6):
            sent(b_slot(j, allz, x, c), b_s.at[j, k], b_r.at[j, k])

    def cols(j):
        return pl.ds(0, width(j))

    def R1(j):
        if j >= 2:
            pl.semaphore_wait(credit_s, 1)
        send(
            ws.at[j, :, :, :, oc, :, cols(j)], l0s.at[j % 2, :, :, :, :, cols(j)],
            r_s.at[j, 0], r_r.at[j, 0], dev_c,
        )

    def add_into(j, count, into, landing, xx):
        def body(zz, carry):
            for k in range(count):
                total = into[j, k, zz, xx, c].astype(F32) + landing[k, zz].astype(F32)
                into[j, k, zz, xx, c] = total.astype(BF16)
            return carry

        lax.fori_loop(0, NZ, body, 0)

    def R2(j):
        slot = j % 2
        got(l0s.at[slot, :, :, :, :, cols(j)], r_s.at[j, 0], r_r.at[j, 0])
        add_into(j, 3, ws, l0s.at[slot, :, :, ox], ox)
        send(
            ws.at[j, :, :, ox, c, :, cols(j)], l1s.at[j, :, :, :, cols(j)],
            r_s.at[j, 1], r_r.at[j, 1], dev_x,
        )
        add_into(j, 3, ws, l0s.at[slot, :, :, x], x)
        if j + 2 < ff_chunks:
            pl.semaphore_signal(credit_s, inc=1, device_id=dev_c, device_id_type=MESH)

    def R3(j):
        got(l1s.at[j, :, :, :, cols(j)], r_s.at[j, 1], r_r.at[j, 1])
        add_into(j, 3, ws, l1s.at[j], x)
        for k in range(3):
            send(
                ws.at[j, :, z_to[k], x, c, :, cols(j)], l2s.at[j, k, :, :, cols(j)],
                r_s.at[j, 2 + k], r_r.at[j, 2 + k], dev_z[k],
            )

    def R4(j):
        for k in range(3):
            got(l2s.at[j, k, :, :, cols(j)], r_s.at[j, 2 + k], r_r.at[j, 2 + k])
        for k in range(3):
            total = ws[j, k, z, x, c].astype(F32)
            for m in range(3):
                total = total + l2s[j, m, k].astype(F32)
            gout_s[j, k] = total
        pltpu.make_async_copy(gout_s.at[j], gs_hbm.at[j], out_sem.at[j]).start()

    def r_sent(j):
        sent(ws.at[j, :, :, :, oc, :, cols(j)], r_s.at[j, 0], r_r.at[j, 0])
        sent(ws.at[j, :, :, ox, c, :, cols(j)], r_s.at[j, 1], r_r.at[j, 1])
        for k in range(3):
            sent(ws.at[j, :, z, x, c, :, cols(j)], r_s.at[j, 2 + k], r_r.at[j, 2 + k])
        pltpu.make_async_copy(gout_s.at[j], gs_hbm.at[j], out_sem.at[j]).wait()

    def Q1(h):
        if h >= 2:
            pl.semaphore_wait(credit_a, 1)
        send(wa.at[h, :, :, :, oc], l0a.at[h % 2], q_s.at[h, 0], q_r.at[h, 0], dev_c)

    def Q2(h):
        slot = h % 2
        got(l0a.at[slot], q_s.at[h, 0], q_r.at[h, 0])
        add_into(h, 4, wa, l0a.at[slot, :, :, ox], ox)
        send(wa.at[h, :, :, ox, c], l1a.at[h], q_s.at[h, 1], q_r.at[h, 1], dev_x)
        add_into(h, 4, wa, l0a.at[slot, :, :, x], x)
        if h + 2 < ATT_CHUNKS:
            pl.semaphore_signal(credit_a, inc=1, device_id=dev_c, device_id_type=MESH)

    def Q3(h):
        got(l1a.at[h], q_s.at[h, 1], q_r.at[h, 1])
        add_into(h, 4, wa, l1a.at[h], x)
        for k in range(3):
            send(
                wa.at[h, :, z_to[k], x, c], l2a.at[h, k],
                q_s.at[h, 2 + k], q_r.at[h, 2 + k], dev_z[k],
            )

    def Q4(h):
        for k in range(3):
            got(l2a.at[h, k], q_s.at[h, 2 + k], q_r.at[h, 2 + k])

        def total(k, col):
            result = wa[h, k, z, x, c, :, col].astype(F32)
            for m in range(3):
                result = result + l2a[h, m, k, :, col].astype(F32)
            return result

        for k in range(4):
            wa[h, k, z, x, c, :, oycol] = total(k, oycol).astype(BF16)
        send(wa.at[h, :, z, x, c, :, oycol], l3a.at[h], q_s.at[h, 5], q_r.at[h, 5], dev_y)
        for k in range(4):
            gout_a[h, k] = total(k, ycol)

    def Q5(h):
        got(l3a.at[h], q_s.at[h, 5], q_r.at[h, 5])
        for k in range(4):
            gout_a[h, k] = gout_a[h, k] + l3a[h, k].astype(F32)
        pltpu.make_async_copy(gout_a.at[h], ga_hbm.at[h], out_sem.at[ff_chunks + h]).start()

    def q_sent(h):
        sent(wa.at[h, :, :, :, oc], q_s.at[h, 0], q_r.at[h, 0])
        sent(wa.at[h, :, :, ox, c], q_s.at[h, 1], q_r.at[h, 1])
        for k in range(3):
            sent(wa.at[h, :, z, x, c], q_s.at[h, 2 + k], q_r.at[h, 2 + k])
        sent(wa.at[h, :, z, x, c, :, oycol], q_s.at[h, 5], q_r.at[h, 5])
        pltpu.make_async_copy(gout_a.at[h], ga_hbm.at[h], out_sem.at[ff_chunks + h]).wait()

    for h in range(ATT_CHUNKS):
        A1(h)
    for j in range(ff_chunks):
        B1(j)

    lanes = lax.broadcasted_iota(jnp.int32, (HALF, HALF), 1)
    low_lane = lanes < ROWS
    half_low = low_lane[:ROWS]
    rows_i = lax.broadcasted_iota(jnp.int32, (ROWS, HALF), 0)
    lane_i = lax.broadcasted_iota(jnp.int32, (ROWS, HALF), 1)
    causal = rows_i <= jnp.where(lane_i < ROWS, lane_i, lane_i - ROWS)
    zero_b = jnp.zeros((HALF, HALF), BF16)
    zero_h = jnp.zeros((ROWS, HALF), BF16)
    scale = float(ROWS) ** (-0.5)

    in_tok.wait()

    def first_norm(i, carry):
        block = pl.ds(pl.multiple_of(i * 64, 64), 64)
        values = tok[block, :].astype(F32)
        in1[block, :] = (values * row_factor(values)).astype(BF16)
        resid[block, :] = values
        return carry

    lax.fori_loop(0, 8, first_norm, 0)
    in_og.wait()

    def clear(i, carry):
        block = pl.ds(pl.multiple_of(i * 64, 64), 64)
        n2b[block, :] = jnp.zeros((64, 1024), F32)
        b2[block, :] = jnp.zeros((64, 1024), F32)
        return carry

    lax.fori_loop(0, 16, clear, 0)
    last = ff_chunks - 1
    if width(last) < WIDE:
        def clear_pad(i, carry):
            for k in range(3):
                for xx in range(2):
                    for cc in range(2):
                        ws[last, k, i, xx, cc, :, pl.ds(HALF, HALF)] = zero_h
            return carry

        lax.fori_loop(0, NZ, clear_pad, 0)

    def transpose_into(dst, src, base, first, count):
        def body(i, carry):
            rows = pl.ds(pl.multiple_of(first + i * HALF, HALF), HALF)
            cols_ = pl.ds(pl.multiple_of(base + i * HALF, HALF), HALF)
            for n in range(8):
                dst[pl.ds(n * HALF, HALF), cols_] = src[rows, pl.ds(n * HALF, HALF)].T
            return carry

        lax.fori_loop(0, count // HALF, body, 0)

    transpose_into(ogt, og, 0, 0, 1024)

    def weight(ref, j, k):
        return ref[j, k].reshape(1024, WIDE)

    def pair_cols(p):
        return pl.ds(p * HALF, HALF)

    def spread(top, mask, zero):
        return jnp.concatenate([jnp.where(mask, top, zero), jnp.where(mask, zero, top)], axis=0)

    def forward_chunk(h):
        def project(tb, carry):
            block = pl.ds(pl.multiple_of(tb * WIDE, WIDE), WIDE)
            left = in1[block, :]
            qb[h, block, :] = dot_nn(left, weight(wa, h, 0)).astype(BF16)
            kb[h, block, :] = dot_nn(left, weight(wa, h, 1)).astype(BF16)
            vb[h, block, :] = dot_nn(left, weight(wa, h, 2)).astype(BF16)
            return carry

        lax.fori_loop(0, 2, project, 0)

        def unit(g, carry):
            block = pl.ds(pl.multiple_of(g * HALF, HALF), HALF)
            for p in range(2):
                col = pair_cols(p)
                k2 = spread(kb[h, block, col], low_lane, zero_b)
                v2 = spread(vb[h, block, col], low_lane, zero_b)
                st = dot_nt(k2, qb[h, block, col])
                pieces = []
                for e in range(2):
                    raw = jnp.where(half_low, st[e * HALF : e * HALF + ROWS], st[e * HALF + ROWS : (e + 1) * HALF])
                    score = jnp.where(causal, raw * scale, -1e30)
                    raised = jnp.exp(score - jnp.max(score, axis=0, keepdims=True))
                    low = (raised / jnp.sum(raised, axis=0, keepdims=True)).astype(BF16)
                    att[h, g, p, pl.ds(e * ROWS, ROWS), :] = low
                    pieces.append(spread(low, half_low, zero_h))
                pt = jnp.concatenate(pieces, axis=0)
                mixed[h, block, col] = dot_tn(pt, v2).astype(BF16)
            return carry

        lax.fori_loop(0, 4, unit, 0)

        def out_project(tb, carry):
            block = pl.ds(pl.multiple_of(tb * WIDE, WIDE), WIDE)
            resid[block, :] = resid[block, :] + dot_nt(mixed[h, block, :], weight(wa, h, 3))
            return carry

        lax.fori_loop(0, 2, out_project, 0)

    def run(table, step, index):
        for key in sorted(table):
            def go(key=key):
                for action, number in table[key]:
                    action(number)
            pl.when(index == key)(go)

    A2(0)
    A2(1)
    A3(0)
    A2(2)
    A3(1)
    A4(0)
    A2(3)
    A3(2)
    A4(1)
    A3(3)
    B2(0)
    before = {
        0: [(A5, 0)],
        1: [(A4, 2), (A5, 1), (B2, 1)],
        2: [(A4, 3), (A5, 2), (B2, 2)],
        3: [(A5, 3), (B2, 3)],
    }

    def attention_step(h, carry):
        run(before, None, h)
        forward_chunk(h)
        return carry

    lax.fori_loop(0, ATT_CHUNKS, attention_step, 0)
    B3(0)

    def second_norm(i, carry):
        block = pl.ds(pl.multiple_of(i * 64, 64), 64)
        values = resid[block, :]
        in2[pl.ds(pl.multiple_of(own + i * 64, 64), 64), :] = (values * row_factor(values)).astype(BF16)
        return carry

    def in2_rows(part, owner):
        return in2.at[pl.ds(owner * 512 + part * 256, 256)]

    for part in range(2):
        lax.fori_loop(part * 4, part * 4 + 4, second_norm, 0)
        send(in2_rows(part, y), in2_rows(part, y), y_s.at[part], y_r.at[part], dev_y)
    transpose_into(in2t, in2, own, own, 512)

    def half_rows(ref, part):
        return ref.at[pl.ds(part * 256, 256)]

    def nsend(part):
        return half_rows(in1, part)

    def bsend(part):
        return in2.at[pl.ds(peer + part * 256, 256)]

    def token_block(j, i):
        is_last = j == last
        first = jnp.where(is_last, 2 * oy, 2 * y)
        index = lax.rem(first + i, 4)
        block = pl.ds(pl.multiple_of(index * WIDE, WIDE), WIDE)
        left = in2[block, :]
        gate = dot_nn(left, weight(ws, j, 0))
        upper = dot_nn(left, weight(ws, j, 1))
        hidden_grad = dot_nn(og[block, :], weight(ws, j, 2))
        hidden = (gate * upper).astype(BF16)
        gate_back = (hidden_grad * upper).astype(BF16)
        up_back = (hidden_grad * gate).astype(BF16)
        hgu[0, block, :] = gate_back
        hgu[1, block, :] = up_back
        hgu[2, block, :] = hidden
        n2b[block, :] = n2b[block, :] + dot_nt(gate_back, weight(ws, j, 0)) + dot_nt(up_back, weight(ws, j, 1))
        b2[block, :] = b2[block, :] + dot_nt(hidden, weight(ws, j, 2))

        for part in range(2):
            def ship(part=part):
                def convert(n, carry):
                    src = pl.ds(pl.multiple_of(peer + part * 256 + n * 64, 64), 64)
                    dst = pl.ds(pl.multiple_of(part * 256 + n * 64, 64), 64)
                    in1[dst, :] = n2b[src, :].astype(BF16)
                    return carry

                lax.fori_loop(0, 4, convert, 0)
                send(nsend(part), half_rows(nland, part), y_s.at[2 + part], y_r.at[2 + part], dev_y)

            pl.when(jnp.logical_and(is_last, i == part))(ship)

    def peer_arrives():
        for part in range(2):
            got(in2_rows(part, oy), y_s.at[part], y_r.at[part])
        transpose_into(in2t, in2, peer, peer, 512)

    def gated_body(j, i, carry):
        pl.when(jnp.logical_and(j == 0, i == 2))(peer_arrives)
        token_block(j, i)
        return carry

    def weight_grads(j):
        def body(r, carry):
            rows = pl.ds(pl.multiple_of(r * WIDE, WIDE), WIDE)
            for k, left in ((0, in2t), (1, in2t), (2, ogt)):
                piece = dot_nn(left[rows, :], hgu[k]).astype(BF16)
                ws[j, k, r] = piece.reshape(2, 2, ROWS, WIDE)
            return carry

        lax.fori_loop(0, NZ, body, 0)

    pre, mid, post = {}, {}, {}
    for j in range(ff_chunks):
        pre[j] = [(B5, j)]
        mid[j] = []
        post[j] = [(R1, j)]
        if j + ATT_CHUNKS < ff_chunks:
            pre[j].insert(0, (B2, j + ATT_CHUNKS))
        if j + 1 < ff_chunks:
            mid[j].append((B3, j + 1))
        mid[j].append((b_sent, j))
        if j >= 1:
            mid[j].append((R2, j - 1))

    def gated_step(j, carry):
        run(pre, None, j)
        lax.fori_loop(0, 4, functools.partial(gated_body, j), 0)
        run(mid, None, j)
        weight_grads(j)
        run(post, None, j)
        return carry

    lax.fori_loop(0, ff_chunks, gated_step, 0)

    for part in range(2):
        sent(in2_rows(part, y), y_s.at[part], y_r.at[part])
    for part in range(2):
        def convert_b(n, carry, part=part):
            src = pl.ds(pl.multiple_of(peer + part * 256 + n * 64, 64), 64)
            in2[src, :] = b2[src, :].astype(BF16)
            return carry

        lax.fori_loop(0, 4, convert_b, 0)
        send(bsend(part), half_rows(bland, part), y_s.at[4 + part], y_r.at[4 + part], dev_y)
    R2(last)

    def first_transposed(i, carry):
        rows = pl.ds(pl.multiple_of(i * HALF, HALF), HALF)
        values = tok[rows, :].astype(F32)
        low = (values * row_factor(values)).astype(BF16)
        for n in range(8):
            in2t[pl.ds(n * HALF, HALF), rows] = low[:, n * HALF : (n + 1) * HALF].T
        return carry

    lax.fori_loop(0, 4, first_transposed, 0)

    for part in range(2):
        got(half_rows(nland, part), y_s.at[2 + part], y_r.at[2 + part])

    def norm_two_back(i, carry):
        block = pl.ds(pl.multiple_of(i * 64, 64), 64)
        mine = pl.ds(pl.multiple_of(own + i * 64, 64), 64)
        other = pl.ds(pl.multiple_of(peer + i * 64, 64), 64)
        values = resid[block, :]
        factor = row_factor(values)
        normed = values * factor
        grad = n2b[mine, :] + nland[block, :].astype(F32)
        back = og[mine, :].astype(F32) + factor * (grad - normed * jnp.mean(grad * normed, axis=-1, keepdims=True))
        n2b[mine, :] = back
        n2b[other, :] = jnp.zeros((64, 1024), F32)
        in2[mine, :] = back.astype(BF16)
        return carry

    lax.fori_loop(0, 8, norm_two_back, 0)
    transpose_into(in2t, in2, 512, own, 512)

    for h in range(ATT_CHUNKS):
        a_sent(h)

    def backward_chunk(h):
        def project(tb, carry):
            block = pl.ds(pl.multiple_of(own + tb * WIDE, WIDE), WIDE)
            hgu[0, pl.ds(pl.multiple_of(512 + tb * WIDE, WIDE), WIDE), :] = dot_nn(
                in2[block, :], weight(wa, h, 3)
            ).astype(BF16)
            return carry

        lax.fori_loop(0, 2, project, 0)

        def unit(g, carry):
            block = pl.ds(pl.multiple_of(g * HALF, HALF), HALF)
            for p in range(2):
                col = pair_cols(p)
                k2 = spread(kb[h, block, col], low_lane, zero_b)
                v2 = spread(vb[h, block, col], low_lane, zero_b)
                back = hgu[0, pl.ds(pl.multiple_of(512 + g * HALF, HALF), HALF), col]
                grads = dot_nt(v2, back)
                kept, changed = [], []
                for e in range(2):
                    low = att[h, g, p, pl.ds(e * ROWS, ROWS), :]
                    wide = low.astype(F32)
                    piece = jnp.where(half_low, grads[e * HALF : e * HALF + ROWS], grads[e * HALF + ROWS : (e + 1) * HALF])
                    inner = jnp.sum(piece * wide, axis=0, keepdims=True)
                    changed.append(spread((wide * (piece - inner)).astype(BF16), half_low, zero_h))
                    kept.append(spread(low, half_low, zero_h))
                pt = jnp.concatenate(kept, axis=0)
                dst = jnp.concatenate(changed, axis=0)
                dv2 = dot_nn(pt, back)
                dk2 = dot_nn(dst, qb[h, block, col])
                hgu[0, block, col] = (scale * dot_tn(dst, k2)).astype(BF16)
                hgu[1, block, col] = (scale * jnp.where(low_lane, dk2[:HALF], dk2[HALF:])).astype(BF16)
                hgu[2, block, col] = jnp.where(low_lane, dv2[:HALF], dv2[HALF:]).astype(BF16)
            return carry

        lax.fori_loop(0, 4, unit, 0)

        def input_grads(tb, carry):
            block = pl.ds(pl.multiple_of(tb * WIDE, WIDE), WIDE)
            into = pl.ds(pl.multiple_of(peer + tb * WIDE, WIDE), WIDE)
            total = n2b[into, :]
            for k in range(3):
                total = total + dot_nt(hgu[k, block, :], weight(wa, h, k))
            n2b[into, :] = total
            return carry

        lax.fori_loop(0, 2, input_grads, 0)

        def weight_part(r, carry):
            rows = pl.ds(pl.multiple_of(r * WIDE, WIDE), WIDE)
            left = in2t[rows, pl.ds(0, 512)]
            for k in range(3):
                wa[h, k, r] = dot_nn(left, hgu[k, pl.ds(0, 512), :]).astype(BF16).reshape(2, 2, ROWS, WIDE)
            wa[h, 3, r] = dot_nn(in2t[rows, pl.ds(512, 512)], mixed[h]).astype(BF16).reshape(2, 2, ROWS, WIDE)
            return carry

        lax.fori_loop(0, NZ, weight_part, 0)

    after = {h: [(Q1, h)] for h in range(ATT_CHUNKS)}
    for h in range(ATT_CHUNKS):
        if h >= 1:
            after[h].append((Q2, h - 1))
        after[h].append((R3, h))
        if h >= 1:
            after[h].append((R4, h - 1))

    def attention_back_step(h, carry):
        backward_chunk(h)
        run(after, None, h)
        return carry

    lax.fori_loop(0, ATT_CHUNKS, attention_back_step, 0)

    for part in range(2):
        sent(nsend(part), y_s.at[2 + part], y_r.at[2 + part])

    def norm_one_back(i, carry):
        block = pl.ds(pl.multiple_of(i * 64, 64), 64)
        mine = pl.ds(pl.multiple_of(own + i * 64, 64), 64)
        other = pl.ds(pl.multiple_of(peer + i * 64, 64), 64)
        values = tok[block, :].astype(F32)
        factor = row_factor(values)
        normed = values * factor
        grad = n2b[other, :]
        back = n2b[mine, :] + factor * (grad - normed * jnp.mean(grad * normed, axis=-1, keepdims=True))
        in1[block, :] = back.astype(BF16)
        return carry

    lax.fori_loop(0, 8, norm_one_back, 0)
    gt_rows = gt_hbm.at[pl.ds(own, 512)]
    send(in1, gt_rows, y_s.at[6], y_r.at[6], dev_y)
    keep_gt = pltpu.make_async_copy(in1, gt_rows, loc_sem.at[0])
    keep_gt.start()
    Q2(ATT_CHUNKS - 1)

    for part in range(2):
        got(half_rows(bland, part), y_s.at[4 + part], y_r.at[4 + part])

    def layer_out(i, carry):
        block = pl.ds(pl.multiple_of(i * 64, 64), 64)
        mine = pl.ds(pl.multiple_of(own + i * 64, 64), 64)
        nland[block, :] = (resid[block, :] + (b2[mine, :] + bland[block, :].astype(F32))).astype(BF16)
        return carry

    lax.fori_loop(0, 8, layer_out, 0)
    bo_rows = bo_hbm.at[pl.ds(own, 512)]
    send(nland, bo_rows, y_s.at[7], y_r.at[7], dev_y)
    keep_bo = pltpu.make_async_copy(nland, bo_rows, loc_sem.at[1])
    keep_bo.start()

    for j in range(ATT_CHUNKS, ff_chunks):
        R3(j)
    for j in range(ATT_CHUNKS - 1, ff_chunks):
        R4(j)
    Q3(0)
    Q3(1)
    Q4(0)
    Q3(2)
    Q4(1)
    Q5(0)
    Q3(3)
    Q4(2)
    Q5(1)
    Q4(3)
    Q5(2)
    Q5(3)

    for part in range(2):
        sent(bsend(part), y_s.at[4 + part], y_r.at[4 + part])
    sent(in1, y_s.at[6], y_r.at[6])
    sent(nland, y_s.at[7], y_r.at[7])
    got(gt_hbm.at[pl.ds(peer, 512)], y_s.at[6], y_r.at[6])
    got(bo_hbm.at[pl.ds(peer, 512)], y_s.at[7], y_r.at[7])
    keep_gt.wait()
    keep_bo.wait()
    for j in range(ff_chunks):
        r_sent(j)
    for h in range(ATT_CHUNKS):
        q_sent(h)


def fast_body(ff_chunks, ff_width, tokens, w_query, w_key, w_value, w_out, w_gate, w_up, w_down, out_grad):
    def attention_shard(matrix):
        return matrix.reshape(ROWS, ATT_CHUNKS, HALF).transpose(1, 0, 2)

    def gated_shard(matrix):
        padded = jnp.pad(matrix, ((0, 0), (0, ff_chunks * WIDE - ff_width)))
        return padded.reshape(ROWS, ff_chunks, WIDE).transpose(1, 0, 2)

    ash = jnp.stack([attention_shard(w) for w in (w_query, w_key, w_value, w_out.T)], axis=1)
    ssh = jnp.stack([gated_shard(w) for w in (w_gate, w_up, w_down.T)], axis=1)
    count, width = tokens.shape
    half = count // 2
    vm = pltpu.VMEM
    dma = pltpu.SemaphoreType.DMA
    scratch = [
        vm((ATT_CHUNKS, 4, NZ, 2, 2, ROWS, WIDE), BF16),
        vm((ff_chunks, 3, NZ, 2, 2, ROWS, WIDE), BF16),
        vm((half, width), BF16),
        vm((half, width), BF16),
        vm((ATT_CHUNKS, half, WIDE), BF16),
        vm((ATT_CHUNKS, half, WIDE), BF16),
        vm((ATT_CHUNKS, half, WIDE), BF16),
        vm((ATT_CHUNKS, half, WIDE), BF16),
        vm((ATT_CHUNKS, 4, 2, HALF, HALF), BF16),
        vm((half, width), F32),
        vm((count, width), BF16),
        vm((width, count), BF16),
        vm((count, width), BF16),
        vm((width, count), BF16),
        vm((count, width), F32),
        vm((count, width), F32),
        vm((3, count, WIDE), BF16),
        vm((half, width), BF16),
        vm((half, width), BF16),
        vm((2, 3, NZ, 2, ROWS, WIDE), BF16),
        vm((ff_chunks, 3, NZ, ROWS, WIDE), BF16),
        vm((ff_chunks, 3, 3, ROWS, WIDE), BF16),
        vm((2, 4, NZ, 2, ROWS, WIDE), BF16),
        vm((ATT_CHUNKS, 4, NZ, ROWS, WIDE), BF16),
        vm((ATT_CHUNKS, 3, 4, ROWS, WIDE), BF16),
        vm((ATT_CHUNKS, 4, ROWS, HALF), BF16),
        vm((ATT_CHUNKS, 4, ROWS, HALF), F32),
        vm((ff_chunks, 3, ROWS, WIDE), F32),
        dma((2 + ATT_CHUNKS + ff_chunks,)),
        dma((ATT_CHUNKS, 10)),
        dma((ATT_CHUNKS, 10)),
        dma((ff_chunks, 6)),
        dma((ff_chunks, 6)),
        dma((ff_chunks, 5)),
        dma((ff_chunks, 5)),
        dma((ATT_CHUNKS, 6)),
        dma((ATT_CHUNKS, 6)),
        dma((8,)),
        dma((8,)),
        dma((ff_chunks + ATT_CHUNKS,)),
        pltpu.SemaphoreType.REGULAR,
        pltpu.SemaphoreType.REGULAR,
    ]
    anywhere = pl.BlockSpec(memory_space=pl.ANY)
    block_out, grad_tokens, ga, gs = pl.pallas_call(
        functools.partial(layer_kernel, ff_chunks, ff_width),
        out_shape=(
            jax.ShapeDtypeStruct((count, width), BF16),
            jax.ShapeDtypeStruct((count, width), BF16),
            jax.ShapeDtypeStruct((ATT_CHUNKS, 4, ROWS, HALF), F32),
            jax.ShapeDtypeStruct((ff_chunks, 3, ROWS, WIDE), F32),
        ),
        in_specs=[anywhere] * 4,
        out_specs=(anywhere,) * 4,
        scratch_shapes=scratch,
        compiler_params=pltpu.CompilerParams(
            collective_id=0, has_side_effects=True, vmem_limit_bytes=67043328
        ),
        name="layer",
    )(tokens, out_grad, ash, ssh)

    def attention_grad(k):
        return ga[:, k].transpose(1, 0, 2).reshape(ROWS, ATT_CHUNKS * HALF)

    def gated_grad(k):
        return gs[:, k].transpose(1, 0, 2).reshape(ROWS, ff_chunks * WIDE)[:, :ff_width]

    return (
        block_out, grad_tokens, attention_grad(0), attention_grad(1), attention_grad(2),
        attention_grad(3).T, gated_grad(0), gated_grad(1), gated_grad(2).T,
    )


def fits(mesh, shapes):
    sizes = dict(mesh.shape)
    tokens, w_query, w_gate = shapes[0], shapes[1], shapes[5]
    return (
        sizes.get("dp") == 16
        and sizes.get("mp") == 2
        and tokens == (16384, 1024)
        and w_query == (1024, 1024)
        and w_gate[1] % (2 * HALF) == 0
        and w_gate[1] // 2 <= 6 * WIDE
    )


def normalize(values_in):
    factor = lax.rsqrt(jnp.mean(values_in * values_in, axis=-1, keepdims=True) + eps)
    return (values_in * factor, factor)


def norm_back(grad_normed, normed, factor):
    return factor * (grad_normed - normed * jnp.mean(grad_normed * normed, axis=-1, keepdims=True))


def contract_rows(left, right):
    return lax.dot_general(
        left, right, (((0,), (0,)), ((), ())), preferred_element_type=jnp.float32
    )


def times_transposed(left, right):
    return lax.dot_general(
        left, right, (((1,), (1,)), ((), ())), preferred_element_type=jnp.float32
    )


def forward_product(left, right):
    return jnp.dot(left, right, preferred_element_type=jnp.float32)


def layer_pass(tokens_part, grad_part, weights):
    w_query, w_key, w_value, w_out, w_gate, w_up, w_down = weights
    count = tokens_part.shape[0]
    width = tokens_part.shape[1]
    head_dim = width // HEADS
    local = w_query.shape[1] // head_dim
    blocks = count // BLK
    scale = head_dim ** (-0.5)
    places = jnp.arange(BLK)
    causal = places[:, None] >= places[None, :]

    def split_heads(matrix):
        return matrix.reshape(blocks, BLK, local, head_dim).transpose(0, 2, 1, 3)

    def join_heads(stacked):
        return stacked.transpose(0, 2, 1, 3).reshape(count, local * head_dim)

    def scores_of(query, keys):
        raw = jnp.einsum("bhqd,bhkd->bhqk", query, keys, preferred_element_type=jnp.float32) * scale
        return jnp.where(causal, raw, -1e30)

    tokens_float = tokens_part.astype(jnp.float32)
    norm_one, factor_one = normalize(tokens_float)
    input_one = norm_one.astype(jnp.bfloat16)
    query = split_heads(forward_product(input_one, w_query).astype(jnp.bfloat16))
    keys = split_heads(forward_product(input_one, w_key).astype(jnp.bfloat16))
    values = split_heads(forward_product(input_one, w_value).astype(jnp.bfloat16))
    scores = scores_of(query, keys)
    peak = jnp.max(scores, axis=-1, keepdims=True)
    raised = jnp.exp(scores - peak)
    totals = jnp.sum(raised, axis=-1, keepdims=True)
    log_total = peak + jnp.log(totals)
    attend_low = (raised / totals).astype(jnp.bfloat16)
    mixed_heads = jnp.einsum(
        "bhqk,bhkd->bhqd", attend_low, values, preferred_element_type=jnp.float32
    )
    mixed = join_heads(mixed_heads.astype(jnp.bfloat16))
    branch_one = lax.psum(forward_product(mixed, w_out), "mp")
    resid = tokens_float + branch_one
    norm_two, factor_two = normalize(resid)
    input_two = norm_two.astype(jnp.bfloat16)
    gate = forward_product(input_two, w_gate)
    upper = forward_product(input_two, w_up)
    hidden = (gate * upper).astype(jnp.bfloat16)
    grad_down = contract_rows(hidden, grad_part)
    grad_hidden = times_transposed(grad_part, w_down)
    gate_back = (grad_hidden * upper).astype(jnp.bfloat16)
    up_back = (grad_hidden * gate).astype(jnp.bfloat16)
    grad_gate = contract_rows(input_two, gate_back)
    grad_up = contract_rows(input_two, up_back)
    two_partial = times_transposed(gate_back, w_gate) + times_transposed(up_back, w_up)
    branch_two = lax.psum(forward_product(hidden, w_down).astype(jnp.bfloat16), "mp").astype(
        jnp.float32
    )
    block_out = (resid + branch_two).astype(jnp.bfloat16)
    norm_two_back = lax.psum(two_partial, "mp")
    resid_back = grad_part.astype(jnp.float32) + norm_back(norm_two_back, norm_two, factor_two)
    branch_back = resid_back.astype(jnp.bfloat16)
    grad_out = contract_rows(mixed, branch_back)
    mixed_back = split_heads(times_transposed(branch_back, w_out).astype(jnp.bfloat16))
    attend = jnp.exp(scores_of(query, keys) - log_total)
    values_back = jnp.einsum(
        "bhqk,bhqd->bhkd", attend_low, mixed_back, preferred_element_type=jnp.float32
    )
    values_back = join_heads(values_back.astype(jnp.bfloat16))
    attend_back = jnp.einsum(
        "bhqd,bhkd->bhqk", mixed_back, values, preferred_element_type=jnp.float32
    )
    scores_back = attend * (attend_back - jnp.sum(attend_back * attend, axis=-1, keepdims=True))
    scores_back = scores_back.astype(jnp.bfloat16)
    query_back = scale * jnp.einsum(
        "bhqk,bhkd->bhqd", scores_back, keys, preferred_element_type=jnp.float32
    )
    query_back = join_heads(query_back.astype(jnp.bfloat16))
    keys_back = scale * jnp.einsum(
        "bhqk,bhqd->bhkd", scores_back, query, preferred_element_type=jnp.float32
    )
    keys_back = join_heads(keys_back.astype(jnp.bfloat16))
    grad_query = contract_rows(input_one, query_back)
    grad_key = contract_rows(input_one, keys_back)
    grad_value = contract_rows(input_one, values_back)
    one_partial = (
        times_transposed(query_back, w_query)
        + times_transposed(keys_back, w_key)
        + times_transposed(values_back, w_value)
    )
    norm_one_back = lax.psum(one_partial, "mp")
    grad_tokens = (resid_back + norm_back(norm_one_back, norm_one, factor_one)).astype(jnp.bfloat16)
    return (
        block_out,
        grad_tokens,
        (grad_query, grad_key, grad_value, grad_out, grad_gate, grad_up, grad_down),
    )


def body(tokens, w_query, w_key, w_value, w_out, w_gate, w_up, w_down, out_grad):
    count = tokens.shape[0] // MICRO
    outputs = []
    backs = []
    summed = None
    for number in range(MICRO):
        weights = (
            lax.all_gather(w_query, "dp", axis=0, tiled=True),
            lax.all_gather(w_key, "dp", axis=0, tiled=True),
            lax.all_gather(w_value, "dp", axis=0, tiled=True),
            lax.all_gather(w_out, "dp", axis=1, tiled=True),
            lax.all_gather(w_gate, "dp", axis=0, tiled=True),
            lax.all_gather(w_up, "dp", axis=0, tiled=True),
            lax.all_gather(w_down, "dp", axis=1, tiled=True),
        )
        first = number * count
        block_out, grad_tokens, grads = layer_pass(
            tokens[first : first + count], out_grad[first : first + count], weights
        )
        outputs.append(block_out)
        backs.append(grad_tokens)
        if number == 0:
            summed = tuple(grads)
        else:
            summed = tuple(jax.tree.map(jnp.add, tuple(summed), tuple(grads)))
    summed = (
        lax.psum_scatter(summed[0], "dp", scatter_dimension=0, tiled=True),
        lax.psum_scatter(summed[1], "dp", scatter_dimension=0, tiled=True),
        lax.psum_scatter(summed[2], "dp", scatter_dimension=0, tiled=True),
        lax.psum_scatter(summed[3], "dp", scatter_dimension=1, tiled=True),
        lax.psum_scatter(summed[4], "dp", scatter_dimension=0, tiled=True),
        lax.psum_scatter(summed[5], "dp", scatter_dimension=0, tiled=True),
        lax.psum_scatter(summed[6], "dp", scatter_dimension=1, tiled=True),
    )
    return (
        jnp.concatenate(outputs, axis=0),
        jnp.concatenate(backs, axis=0),
        summed[0],
        summed[1],
        summed[2],
        summed[3],
        summed[4],
        summed[5],
        summed[6],
    )


def solution(mesh):
    in_specs = (
        P("dp", None),
        P("dp", "mp"),
        P("dp", "mp"),
        P("dp", "mp"),
        P("mp", "dp"),
        P("dp", "mp"),
        P("dp", "mp"),
        P("mp", "dp"),
        P("dp", None),
    )
    out_specs = (
        P("dp", None),
        P("dp", None),
        P("dp", "mp"),
        P("dp", "mp"),
        P("dp", "mp"),
        P("mp", "dp"),
        P("dp", "mp"),
        P("dp", "mp"),
        P("mp", "dp"),
    )

    def program(*args):
        shapes = [a.shape for a in args]
        if fits(mesh, shapes):
            ff_width = shapes[5][1] // 2
            chosen = functools.partial(fast_body, pl.cdiv(ff_width, WIDE), ff_width)
        else:
            chosen = body
        return jax.shard_map(
            chosen, mesh=mesh, in_specs=in_specs, out_specs=out_specs, check_vma=False
        )(*args)

    return program
```

```python
import functools

import jax
import jax.numpy as jnp
from jax import lax
from jax.experimental import pallas as pl
from jax.experimental.pallas import tpu as pltpu
from jax.sharding import PartitionSpec as P

HEADS = 16
BLK = 64
MICRO = 2

eps = 1e-06

F32 = jnp.float32
BF16 = jnp.bfloat16
MESH = pl.DeviceIdType.MESH
NZ = 4
HALF = 128
WIDE = 256
ATT_CHUNKS = 4
ROWS = 64


def dot_nn(left, right):
    return lax.dot_general(left, right, (((1,), (0,)), ((), ())), preferred_element_type=F32)


def dot_nt(left, right):
    return lax.dot_general(left, right, (((1,), (1,)), ((), ())), preferred_element_type=F32)


def dot_tn(left, right):
    return lax.dot_general(left, right, (((0,), (0,)), ((), ())), preferred_element_type=F32)


def row_factor(values):
    return lax.rsqrt(jnp.mean(values * values, axis=-1, keepdims=True) + eps)


def layer_kernel(
    ff_chunks, ff_width,
    tok_hbm, og_hbm, ash, ssh,
    bo_hbm, gt_hbm, ga_hbm, gs_hbm,
    wa, ws, tok, in1, qb, kb, vb, mixed, att, resid, in2, in2t, og, ogt, nown, bown, pacc, hgu,
    nland, bland, l0, l1s, l2s, l1a, l2a, l3a, gout_a, gout_s,
    loc_sem, a_s, a_r, b_s, b_r, r_s, r_r, q_s, q_r, y_s, y_r, out_sem, credit,
):
    dp = lax.axis_index("dp")
    y = lax.axis_index("mp")
    z = lax.div(dp, 4)
    x = lax.rem(lax.div(dp, 2), 2)
    c = lax.rem(dp, 2)
    ox, oy, oc = 1 - x, 1 - y, 1 - c

    def at_dev(zz, xx, cc, yy):
        return (zz * 4 + xx * 2 + cc, yy)

    dev_x = at_dev(z, ox, c, y)
    dev_y = at_dev(z, x, c, oy)
    dev_c = at_dev(z, x, oc, y)
    z_to = [lax.rem(z + k, NZ) for k in (1, 2, 3)]
    z_from = [lax.rem(z + NZ - k, NZ) for k in (1, 2, 3)]
    dev_z = [at_dev(t, x, c, y) for t in z_to]

    def remote(src, dst, ssem, rsem, device):
        return pltpu.make_async_remote_copy(
            src_ref=src, dst_ref=dst, send_sem=ssem, recv_sem=rsem,
            device_id=device, device_id_type=MESH,
        )

    def send(src, dst, ssem, rsem, device):
        remote(src, dst, ssem, rsem, device).start()

    def got(dst, ssem, rsem):
        remote(dst, dst, ssem, rsem, dev_c).wait_recv()

    def sent(src, ssem, rsem):
        remote(src, src, ssem, rsem, dev_c).wait_send()

    barrier = pltpu.get_barrier_semaphore()
    for device in [dev_c, dev_x, dev_y] + dev_z:
        pl.semaphore_signal(barrier, inc=1, device_id=device, device_id_type=MESH)

    own = y * 512
    peer = oy * 512
    in_tok = pltpu.make_async_copy(tok_hbm.at[pl.ds(own, 512)], tok, loc_sem.at[0])
    in_og = pltpu.make_async_copy(og_hbm, og, loc_sem.at[1])
    in_tok.start()
    in_og.start()
    pl.semaphore_wait(barrier, 6)

    ycol = pl.ds(y * HALF, HALF)
    oycol = pl.ds(oy * HALF, HALF)

    def a_slot(h, zz, xx, cc, col):
        return wa.at[h, :, zz, xx, cc, :, col]

    allz = slice(None)

    def A1(h):
        for k in range(3):
            send(ash.at[h], a_slot(h, z, x, c, ycol), a_s.at[h, k], a_r.at[h, k], dev_z[k])
        pltpu.make_async_copy(ash.at[h], a_slot(h, z, x, c, ycol), loc_sem.at[2 + h]).start()

    def A2(h):
        for k in range(3):
            got(a_slot(h, z_from[k], x, c, ycol), a_s.at[h, k], a_r.at[h, k])
        pltpu.make_async_copy(ash.at[h], a_slot(h, z, x, c, ycol), loc_sem.at[2 + h]).wait()
        mine = a_slot(h, allz, x, c, ycol)
        first, second = (dev_x, dev_y) if h % 2 == 0 else (dev_y, dev_x)
        send(mine, mine, a_s.at[h, 3], a_r.at[h, 3], first)
        send(mine, mine, a_s.at[h, 4], a_r.at[h, 4], second)
        send(mine, mine, a_s.at[h, 6], a_r.at[h, 6], dev_c)

    def a_from_x(h):
        return a_slot(h, allz, ox, c, ycol)

    def a_from_y(h):
        return a_slot(h, allz, x, c, oycol)

    def a_first(h):
        return a_from_x(h) if h % 2 == 0 else a_from_y(h)

    def a_second(h):
        return a_from_y(h) if h % 2 == 0 else a_from_x(h)

    def a_corner(h):
        return a_slot(h, allz, ox, c, oycol)

    def A3(h):
        got(a_first(h), a_s.at[h, 3], a_r.at[h, 3])
        second = dev_y if h % 2 == 0 else dev_x
        part = a_first(h)
        send(part, part, a_s.at[h, 5], a_r.at[h, 5], second)
        send(part, part, a_s.at[h, 7], a_r.at[h, 7], dev_c)

    def A4(h):
        got(a_second(h), a_s.at[h, 4], a_r.at[h, 4])
        part = a_second(h)
        send(part, part, a_s.at[h, 8], a_r.at[h, 8], dev_c)
        got(a_corner(h), a_s.at[h, 5], a_r.at[h, 5])
        part = a_corner(h)
        send(part, part, a_s.at[h, 9], a_r.at[h, 9], dev_c)

    def A5(h):
        part = a_slot(h, allz, x, oc, ycol)
        for k in range(6, 10):
            got(part, a_s.at[h, k], a_r.at[h, k])

    def a_sent(h):
        for k in range(3):
            sent(ash.at[h], a_s.at[h, k], a_r.at[h, k])
        mine = a_slot(h, allz, x, c, ycol)
        for k in range(3, 10):
            sent(mine, a_s.at[h, k], a_r.at[h, k])

    def width(j):
        return min(WIDE, ff_width - j * WIDE)

    def b_slot(j, zz, xx, cc):
        return ws.at[j, :, zz, xx, cc, :, pl.ds(0, width(j))]

    def b_shard(j):
        return ssh.at[j, :, :, pl.ds(0, width(j))]

    def B1(j):
        for k in range(3):
            send(b_shard(j), b_slot(j, z, x, c), b_s.at[j, k], b_r.at[j, k], dev_z[k])
        pltpu.make_async_copy(b_shard(j), b_slot(j, z, x, c), loc_sem.at[2 + ATT_CHUNKS + j]).start()

    def B2(j):
        for k in range(3):
            got(b_slot(j, z_from[k], x, c), b_s.at[j, k], b_r.at[j, k])
        pltpu.make_async_copy(b_shard(j), b_slot(j, z, x, c), loc_sem.at[2 + ATT_CHUNKS + j]).wait()
        mine = b_slot(j, allz, x, c)
        send(mine, mine, b_s.at[j, 3], b_r.at[j, 3], dev_x)
        send(mine, mine, b_s.at[j, 4], b_r.at[j, 4], dev_c)

    def B3(j):
        part = b_slot(j, allz, ox, c)
        got(part, b_s.at[j, 3], b_r.at[j, 3])
        send(part, part, b_s.at[j, 5], b_r.at[j, 5], dev_c)

    def B5(j):
        got(b_slot(j, allz, x, oc), b_s.at[j, 4], b_r.at[j, 4])
        got(b_slot(j, allz, ox, oc), b_s.at[j, 5], b_r.at[j, 5])

    def b_sent(j):
        for k in range(3):
            sent(b_shard(j), b_s.at[j, k], b_r.at[j, k])
        for k in range(3, 6):
            sent(b_slot(j, allz, x, c), b_s.at[j, k], b_r.at[j, k])

    def cols(j):
        return pl.ds(0, width(j))

    def R1(j):
        if j >= 2:
            pl.semaphore_wait(credit, 1)
        send(
            ws.at[j, :, :, :, oc, :, cols(j)], l0.at[j % 2, pl.ds(0, 3), :, :, :, cols(j)],
            r_s.at[j, 0], r_r.at[j, 0], dev_c,
        )

    def add_into(j, count, into, landing, xx):
        def body(zz, carry):
            for k in range(count):
                total = into[j, k, zz, xx, c].astype(F32) + landing[k, zz].astype(F32)
                into[j, k, zz, xx, c] = total.astype(BF16)
            return carry

        lax.fori_loop(0, NZ, body, 0)

    def R2(j):
        slot = j % 2
        got(l0.at[slot, pl.ds(0, 3), :, :, :, cols(j)], r_s.at[j, 0], r_r.at[j, 0])
        add_into(j, 3, ws, l0.at[slot, :, :, ox], ox)
        send(
            ws.at[j, :, :, ox, c, :, cols(j)], l1s.at[j, :, :, :, cols(j)],
            r_s.at[j, 1], r_r.at[j, 1], dev_x,
        )
        add_into(j, 3, ws, l0.at[slot, :, :, x], x)
        if j + 2 < ff_chunks + ATT_CHUNKS:
            pl.semaphore_signal(credit, inc=1, device_id=dev_c, device_id_type=MESH)

    def R3(j):
        got(l1s.at[j, :, :, :, cols(j)], r_s.at[j, 1], r_r.at[j, 1])
        add_into(j, 3, ws, l1s.at[j], x)
        for k in range(3):
            send(
                ws.at[j, :, z_to[k], x, c, :, cols(j)], l2s.at[j, k, :, :, cols(j)],
                r_s.at[j, 2 + k], r_r.at[j, 2 + k], dev_z[k],
            )

    def R4(j):
        for k in range(3):
            got(l2s.at[j, k, :, :, cols(j)], r_s.at[j, 2 + k], r_r.at[j, 2 + k])
        for k in range(3):
            total = ws[j, k, z, x, c].astype(F32)
            for m in range(3):
                total = total + l2s[j, m, k].astype(F32)
            gout_s[j, k] = total
        pltpu.make_async_copy(gout_s.at[j], gs_hbm.at[j], out_sem.at[j]).start()

    def r_sent(j):
        sent(ws.at[j, :, :, :, oc, :, cols(j)], r_s.at[j, 0], r_r.at[j, 0])
        sent(ws.at[j, :, :, ox, c, :, cols(j)], r_s.at[j, 1], r_r.at[j, 1])
        for k in range(3):
            sent(ws.at[j, :, z, x, c, :, cols(j)], r_s.at[j, 2 + k], r_r.at[j, 2 + k])
        pltpu.make_async_copy(gout_s.at[j], gs_hbm.at[j], out_sem.at[j]).wait()

    def Q1(h):
        if ff_chunks + h >= 2:
            pl.semaphore_wait(credit, 1)
        send(wa.at[h, :, :, :, oc], l0.at[(ff_chunks + h) % 2], q_s.at[h, 0], q_r.at[h, 0], dev_c)

    def Q2(h):
        slot = (ff_chunks + h) % 2
        got(l0.at[slot], q_s.at[h, 0], q_r.at[h, 0])
        add_into(h, 4, wa, l0.at[slot, :, :, ox], ox)
        send(wa.at[h, :, :, ox, c], l1a.at[h], q_s.at[h, 1], q_r.at[h, 1], dev_x)
        add_into(h, 4, wa, l0.at[slot, :, :, x], x)
        if h + 2 < ATT_CHUNKS:
            pl.semaphore_signal(credit, inc=1, device_id=dev_c, device_id_type=MESH)

    def Q3(h):
        got(l1a.at[h], q_s.at[h, 1], q_r.at[h, 1])
        add_into(h, 4, wa, l1a.at[h], x)
        for k in range(3):
            send(
                wa.at[h, :, z_to[k], x, c], l2a.at[h, k],
                q_s.at[h, 2 + k], q_r.at[h, 2 + k], dev_z[k],
            )

    def Q4(h):
        for k in range(3):
            got(l2a.at[h, k], q_s.at[h, 2 + k], q_r.at[h, 2 + k])

        def total(k, col):
            result = wa[h, k, z, x, c, :, col].astype(F32)
            for m in range(3):
                result = result + l2a[h, m, k, :, col].astype(F32)
            return result

        for k in range(4):
            wa[h, k, z, x, c, :, oycol] = total(k, oycol).astype(BF16)
        send(wa.at[h, :, z, x, c, :, oycol], l3a.at[h], q_s.at[h, 5], q_r.at[h, 5], dev_y)
        for k in range(4):
            gout_a[h, k] = total(k, ycol)

    def Q5(h):
        got(l3a.at[h], q_s.at[h, 5], q_r.at[h, 5])
        for k in range(4):
            gout_a[h, k] = gout_a[h, k] + l3a[h, k].astype(F32)
        pltpu.make_async_copy(gout_a.at[h], ga_hbm.at[h], out_sem.at[ff_chunks + h]).start()

    def q_sent(h):
        sent(wa.at[h, :, :, :, oc], q_s.at[h, 0], q_r.at[h, 0])
        sent(wa.at[h, :, :, ox, c], q_s.at[h, 1], q_r.at[h, 1])
        for k in range(3):
            sent(wa.at[h, :, z, x, c], q_s.at[h, 2 + k], q_r.at[h, 2 + k])
        sent(wa.at[h, :, z, x, c, :, oycol], q_s.at[h, 5], q_r.at[h, 5])
        pltpu.make_async_copy(gout_a.at[h], ga_hbm.at[h], out_sem.at[ff_chunks + h]).wait()

    for h in range(ATT_CHUNKS):
        A1(h)

    lanes = lax.broadcasted_iota(jnp.int32, (HALF, HALF), 1)
    low_lane = lanes < ROWS
    half_low = low_lane[:ROWS]
    rows_i = lax.broadcasted_iota(jnp.int32, (ROWS, HALF), 0)
    lane_i = lax.broadcasted_iota(jnp.int32, (ROWS, HALF), 1)
    causal = rows_i <= jnp.where(lane_i < ROWS, lane_i, lane_i - ROWS)
    zero_b = jnp.zeros((HALF, HALF), BF16)
    zero_h = jnp.zeros((ROWS, HALF), BF16)
    scale = float(ROWS) ** (-0.5)

    in_tok.wait()

    def first_norm(i, carry):
        block = pl.ds(pl.multiple_of(i * 64, 64), 64)
        values = tok[block, :].astype(F32)
        in1[block, :] = (values * row_factor(values)).astype(BF16)
        resid[block, :] = values
        return carry

    lax.fori_loop(0, 8, first_norm, 0)
    def clear(i, carry):
        block = pl.ds(pl.multiple_of(i * 64, 64), 64)
        nown[block, :] = jnp.zeros((64, 1024), F32)
        bown[block, :] = jnp.zeros((64, 1024), F32)
        return carry

    last = ff_chunks - 1

    def clear_pad(i, carry):
        for k in range(3):
            for xx in range(2):
                for cc in range(2):
                    ws[last, k, i, xx, cc, :, pl.ds(HALF, HALF)] = zero_h
        return carry

    def transpose_into(dst, src, base, first, count):
        def body(i, carry):
            rows = pl.ds(pl.multiple_of(first + i * HALF, HALF), HALF)
            cols_ = pl.ds(pl.multiple_of(base + i * HALF, HALF), HALF)
            for n in range(8):
                dst[pl.ds(n * HALF, HALF), cols_] = src[rows, pl.ds(n * HALF, HALF)].T
            return carry

        lax.fori_loop(0, count // HALF, body, 0)

    def weight(ref, j, k):
        return ref[j, k].reshape(1024, WIDE)

    def pair_cols(p):
        return pl.ds(p * HALF, HALF)

    def spread(top, mask, zero):
        return jnp.concatenate([jnp.where(mask, top, zero), jnp.where(mask, zero, top)], axis=0)

    def forward_chunk(h):
        def project(tb, carry):
            block = pl.ds(pl.multiple_of(tb * WIDE, WIDE), WIDE)
            left = in1[block, :]
            qb[h, block, :] = dot_nn(left, weight(wa, h, 0)).astype(BF16)
            kb[h, block, :] = dot_nn(left, weight(wa, h, 1)).astype(BF16)
            vb[h, block, :] = dot_nn(left, weight(wa, h, 2)).astype(BF16)
            return carry

        lax.fori_loop(0, 2, project, 0)

        def unit(g, carry):
            block = pl.ds(pl.multiple_of(g * HALF, HALF), HALF)
            for p in range(2):
                col = pair_cols(p)
                k2 = spread(kb[h, block, col], low_lane, zero_b)
                v2 = spread(vb[h, block, col], low_lane, zero_b)
                st = dot_nt(k2, qb[h, block, col])
                pieces = []
                for e in range(2):
                    raw = jnp.where(half_low, st[e * HALF : e * HALF + ROWS], st[e * HALF + ROWS : (e + 1) * HALF])
                    score = jnp.where(causal, raw * scale, -1e30)
                    raised = jnp.exp(score - jnp.max(score, axis=0, keepdims=True))
                    low = (raised / jnp.sum(raised, axis=0, keepdims=True)).astype(BF16)
                    att[h, g, p, pl.ds(e * ROWS, ROWS), :] = low
                    pieces.append(spread(low, half_low, zero_h))
                pt = jnp.concatenate(pieces, axis=0)
                mixed[h, block, col] = dot_tn(pt, v2).astype(BF16)
            return carry

        lax.fori_loop(0, 4, unit, 0)

        def out_project(tb, carry):
            block = pl.ds(pl.multiple_of(tb * WIDE, WIDE), WIDE)
            resid[block, :] = resid[block, :] + dot_nt(mixed[h, block, :], weight(wa, h, 3))
            return carry

        lax.fori_loop(0, 2, out_project, 0)

    def run(table, step, index):
        for key in sorted(table):
            def go(key=key):
                for action, number in table[key]:
                    action(number)
            pl.when(index == key)(go)

    A2(0)
    for j in range(ff_chunks):
        B1(j)
    A2(1)
    A3(0)
    lax.fori_loop(0, 8, clear, 0)
    if width(last) < WIDE:
        lax.fori_loop(0, NZ, clear_pad, 0)
    A2(2)
    A3(1)
    A4(0)
    in_og.wait()
    transpose_into(ogt, og, 0, 0, 512)
    A2(3)
    A3(2)
    A4(1)
    transpose_into(ogt, og, 512, 512, 512)
    A3(3)
    B2(0)
    before = {
        0: [(A5, 0)],
        1: [(A4, 2), (A5, 1), (B2, 1)],
        2: [(A4, 3), (A5, 2), (B2, 2)],
        3: [(A5, 3), (B2, 3)],
    }

    def attention_step(h, carry):
        run(before, None, h)
        forward_chunk(h)
        return carry

    lax.fori_loop(0, ATT_CHUNKS, attention_step, 0)
    B3(0)

    def second_norm(i, carry):
        block = pl.ds(pl.multiple_of(i * 64, 64), 64)
        values = resid[block, :]
        in2[pl.ds(pl.multiple_of(own + i * 64, 64), 64), :] = (values * row_factor(values)).astype(BF16)
        return carry

    def in2_rows(part, owner):
        return in2.at[pl.ds(owner * 512 + part * 256, 256)]

    for part in range(2):
        lax.fori_loop(part * 4, part * 4 + 4, second_norm, 0)
        send(in2_rows(part, y), in2_rows(part, y), y_s.at[part], y_r.at[part], dev_y)
    transpose_into(in2t, in2, own, own, 512)

    def half_rows(ref, part):
        return ref.at[pl.ds(part * 256, 256)]

    def nsend(part):
        return half_rows(in1, part)

    def bsend(part):
        return in2.at[pl.ds(peer + part * 256, 256)]

    def gated_block(j, block):
        left = in2[block, :]
        gate = dot_nn(left, weight(ws, j, 0))
        upper = dot_nn(left, weight(ws, j, 1))
        hidden_grad = dot_nn(og[block, :], weight(ws, j, 2))
        hidden = (gate * upper).astype(BF16)
        gate_back = (hidden_grad * upper).astype(BF16)
        up_back = (hidden_grad * gate).astype(BF16)
        hgu[0, j, block, :] = gate_back
        hgu[1, j, block, :] = up_back
        hgu[2, j, block, :] = hidden
        norm_part = dot_nt(gate_back, weight(ws, j, 0)) + dot_nt(up_back, weight(ws, j, 1))
        return norm_part, dot_nt(hidden, weight(ws, j, 2))

    pre, mid, post = {}, {}, {}
    for j in range(ff_chunks):
        pre[j] = [(B5, j)]
        mid[j] = []
        post[j] = [(R1, j)]
        if j + ATT_CHUNKS < ff_chunks:
            pre[j].insert(0, (B2, j + ATT_CHUNKS))
        if j + 1 < ff_chunks:
            mid[j].append((B3, j + 1))
        if j >= 1:
            post[j].append((R2, j - 1))

    def own_pass(j, carry):
        run(pre, None, j)

        def body(i, inner):
            rows = pl.ds(pl.multiple_of(i * WIDE, WIDE), WIDE)
            norm_part, branch_part = gated_block(j, pl.ds(pl.multiple_of(own + i * WIDE, WIDE), WIDE))
            nown[rows, :] = nown[rows, :] + norm_part
            bown[rows, :] = bown[rows, :] + branch_part
            return inner

        lax.fori_loop(0, 2, body, 0)
        run(mid, None, j)
        return carry

    lax.fori_loop(0, ff_chunks, own_pass, 0)

    def peer_pass(part, carry):
        got(in2_rows(part, oy), y_s.at[part], y_r.at[part])
        block = pl.ds(pl.multiple_of(peer + part * WIDE, WIDE), WIDE)

        def zero(n, inner):
            rows = pl.ds(pl.multiple_of(n * 64, 64), 64)
            pacc[0, rows, :] = jnp.zeros((64, 1024), F32)
            pacc[1, rows, :] = jnp.zeros((64, 1024), F32)
            return inner

        lax.fori_loop(0, 4, zero, 0)

        def body(j, inner):
            norm_part, branch_part = gated_block(j, block)
            pacc[0] = pacc[0] + norm_part
            pacc[1] = pacc[1] + branch_part
            return inner

        lax.fori_loop(0, ff_chunks, body, 0)

        def convert(n, inner):
            src = pl.ds(pl.multiple_of(n * 64, 64), 64)
            in1[pl.ds(pl.multiple_of(part * WIDE + n * 64, 64), 64), :] = pacc[0, src, :].astype(BF16)
            return inner

        lax.fori_loop(0, 4, convert, 0)
        send(nsend(part), half_rows(nland, part), y_s.at[2 + part], y_r.at[2 + part], dev_y)
        transpose_into(in2t, in2, peer + part * WIDE, peer + part * WIDE, WIDE)

        def convert_b(n, inner):
            src = pl.ds(pl.multiple_of(n * 64, 64), 64)
            in2[pl.ds(pl.multiple_of(peer + part * WIDE + n * 64, 64), 64), :] = pacc[1, src, :].astype(BF16)
            return inner

        lax.fori_loop(0, 4, convert_b, 0)
        return carry

    lax.fori_loop(0, 2, peer_pass, 0)
    for part in range(2):
        send(bsend(part), half_rows(bland, part), y_s.at[4 + part], y_r.at[4 + part], dev_y)
        sent(in2_rows(part, y), y_s.at[part], y_r.at[part])
    for j in range(ff_chunks):
        b_sent(j)

    def weight_grads(j):
        def body(r, carry):
            rows = pl.ds(pl.multiple_of(r * WIDE, WIDE), WIDE)
            for k, left in ((0, in2t), (1, in2t), (2, ogt)):
                piece = dot_nn(left[rows, :], hgu[k, j]).astype(BF16)
                ws[j, k, r] = piece.reshape(2, 2, ROWS, WIDE)
            return carry

        lax.fori_loop(0, NZ, body, 0)

    def grads_step(j, carry):
        weight_grads(j)
        run(post, None, j)
        return carry

    lax.fori_loop(0, ff_chunks, grads_step, 0)
    R2(last)

    def first_transposed(i, carry):
        rows = pl.ds(pl.multiple_of(i * HALF, HALF), HALF)
        values = tok[rows, :].astype(F32)
        low = (values * row_factor(values)).astype(BF16)
        for n in range(8):
            in2t[pl.ds(n * HALF, HALF), rows] = low[:, n * HALF : (n + 1) * HALF].T
        return carry

    lax.fori_loop(0, 4, first_transposed, 0)

    for part in range(2):
        got(half_rows(nland, part), y_s.at[2 + part], y_r.at[2 + part])

    def norm_two_back(i, carry):
        block = pl.ds(pl.multiple_of(i * 64, 64), 64)
        mine = pl.ds(pl.multiple_of(own + i * 64, 64), 64)
        values = resid[block, :]
        factor = row_factor(values)
        normed = values * factor
        grad = nown[block, :] + nland[block, :].astype(F32)
        back = og[mine, :].astype(F32) + factor * (grad - normed * jnp.mean(grad * normed, axis=-1, keepdims=True))
        nown[block, :] = back
        in2[mine, :] = back.astype(BF16)
        return carry

    lax.fori_loop(0, 8, norm_two_back, 0)

    def zero_acc(n, carry):
        rows = pl.ds(pl.multiple_of(n * 64, 64), 64)
        for part in range(2):
            pacc[part, rows, :] = jnp.zeros((64, 1024), F32)
        return carry

    lax.fori_loop(0, 4, zero_acc, 0)
    transpose_into(in2t, in2, 512, own, 512)

    for h in range(ATT_CHUNKS):
        a_sent(h)

    def backward_chunk(h):
        def project(tb, carry):
            block = pl.ds(pl.multiple_of(own + tb * WIDE, WIDE), WIDE)
            hgu[0, 0, pl.ds(pl.multiple_of(512 + tb * WIDE, WIDE), WIDE), :] = dot_nn(
                in2[block, :], weight(wa, h, 3)
            ).astype(BF16)
            return carry

        lax.fori_loop(0, 2, project, 0)

        def unit(g, carry):
            block = pl.ds(pl.multiple_of(g * HALF, HALF), HALF)
            for p in range(2):
                col = pair_cols(p)
                k2 = spread(kb[h, block, col], low_lane, zero_b)
                v2 = spread(vb[h, block, col], low_lane, zero_b)
                back = hgu[0, 0, pl.ds(pl.multiple_of(512 + g * HALF, HALF), HALF), col]
                grads = dot_nt(v2, back)
                kept, changed = [], []
                for e in range(2):
                    low = att[h, g, p, pl.ds(e * ROWS, ROWS), :]
                    wide = low.astype(F32)
                    piece = jnp.where(half_low, grads[e * HALF : e * HALF + ROWS], grads[e * HALF + ROWS : (e + 1) * HALF])
                    inner = jnp.sum(piece * wide, axis=0, keepdims=True)
                    changed.append(spread((wide * (piece - inner)).astype(BF16), half_low, zero_h))
                    kept.append(spread(low, half_low, zero_h))
                pt = jnp.concatenate(kept, axis=0)
                dst = jnp.concatenate(changed, axis=0)
                dv2 = dot_nn(pt, back)
                dk2 = dot_nn(dst, qb[h, block, col])
                hgu[0, 0, block, col] = (scale * dot_tn(dst, k2)).astype(BF16)
                hgu[1, 0, block, col] = (scale * jnp.where(low_lane, dk2[:HALF], dk2[HALF:])).astype(BF16)
                hgu[2, 0, block, col] = jnp.where(low_lane, dv2[:HALF], dv2[HALF:]).astype(BF16)
            return carry

        lax.fori_loop(0, 4, unit, 0)

        def input_grads(tb, carry):
            block = pl.ds(pl.multiple_of(tb * WIDE, WIDE), WIDE)
            total = pacc[tb]
            for k in range(3):
                total = total + dot_nt(hgu[k, 0, block, :], weight(wa, h, k))
            pacc[tb] = total
            return carry

        lax.fori_loop(0, 2, input_grads, 0)

        def weight_part(r, carry):
            rows = pl.ds(pl.multiple_of(r * WIDE, WIDE), WIDE)
            left = in2t[rows, pl.ds(0, 512)]
            for k in range(3):
                wa[h, k, r] = dot_nn(left, hgu[k, 0, pl.ds(0, 512), :]).astype(BF16).reshape(2, 2, ROWS, WIDE)
            wa[h, 3, r] = dot_nn(in2t[rows, pl.ds(512, 512)], mixed[h]).astype(BF16).reshape(2, 2, ROWS, WIDE)
            return carry

        lax.fori_loop(0, NZ, weight_part, 0)

    bo_rows = bo_hbm.at[pl.ds(own, 512)]

    def emit_out(_):
        for part in range(2):
            got(half_rows(bland, part), y_s.at[4 + part], y_r.at[4 + part])

        def layer_out(i, carry):
            block = pl.ds(pl.multiple_of(i * 64, 64), 64)
            nland[block, :] = (resid[block, :] + (bown[block, :] + bland[block, :].astype(F32))).astype(BF16)
            return carry

        lax.fori_loop(0, 8, layer_out, 0)
        send(nland, bo_rows, y_s.at[7], y_r.at[7], dev_y)
        pltpu.make_async_copy(nland, bo_rows, loc_sem.at[1]).start()

    after = {
        0: [(Q1, 0), (R3, 1), (R3, 2)],
        1: [(Q1, 1), (Q2, 0), (R3, 3), (R4, 0), (R4, 1)],
        2: [(Q1, 2), (Q2, 1), (R3, 4), (R4, 2), (emit_out, 0)],
        3: [(Q1, 3), (Q2, 2)],
    }
    R3(0)

    def attention_back_step(h, carry):
        backward_chunk(h)
        run(after, None, h)
        return carry

    lax.fori_loop(0, ATT_CHUNKS, attention_back_step, 0)

    for part in range(2):
        sent(nsend(part), y_s.at[2 + part], y_r.at[2 + part])

    def norm_one_back(i, carry):
        block = pl.ds(pl.multiple_of(i * 64, 64), 64)
        values = tok[block, :].astype(F32)
        factor = row_factor(values)
        normed = values * factor
        grad = pacc[lax.div(i, 4), pl.ds(pl.multiple_of(lax.rem(i, 4) * 64, 64), 64), :]
        back = nown[block, :] + factor * (grad - normed * jnp.mean(grad * normed, axis=-1, keepdims=True))
        in1[block, :] = back.astype(BF16)
        return carry

    lax.fori_loop(0, 8, norm_one_back, 0)
    gt_rows = gt_hbm.at[pl.ds(own, 512)]
    send(in1, gt_rows, y_s.at[6], y_r.at[6], dev_y)
    keep_gt = pltpu.make_async_copy(in1, gt_rows, loc_sem.at[0])
    keep_gt.start()
    Q2(ATT_CHUNKS - 1)

    R3(5)
    for j in range(3, ff_chunks):
        R4(j)
    Q3(0)
    Q3(1)
    Q4(0)
    Q3(2)
    Q4(1)
    Q5(0)
    Q3(3)
    Q4(2)
    Q5(1)
    Q4(3)
    Q5(2)
    Q5(3)

    for part in range(2):
        sent(bsend(part), y_s.at[4 + part], y_r.at[4 + part])
    sent(in1, y_s.at[6], y_r.at[6])
    sent(nland, y_s.at[7], y_r.at[7])
    got(gt_hbm.at[pl.ds(peer, 512)], y_s.at[6], y_r.at[6])
    got(bo_hbm.at[pl.ds(peer, 512)], y_s.at[7], y_r.at[7])
    keep_gt.wait()
    pltpu.make_async_copy(nland, bo_rows, loc_sem.at[1]).wait()
    for j in range(ff_chunks):
        r_sent(j)
    for h in range(ATT_CHUNKS):
        q_sent(h)


def fast_body(ff_chunks, ff_width, tokens, w_query, w_key, w_value, w_out, w_gate, w_up, w_down, out_grad):
    def attention_shard(matrix):
        return matrix.reshape(ROWS, ATT_CHUNKS, HALF).transpose(1, 0, 2)

    def gated_shard(matrix):
        padded = jnp.pad(matrix, ((0, 0), (0, ff_chunks * WIDE - ff_width)))
        return padded.reshape(ROWS, ff_chunks, WIDE).transpose(1, 0, 2)

    ash = jnp.stack([attention_shard(w) for w in (w_query, w_key, w_value, w_out.T)], axis=1)
    ssh = jnp.stack([gated_shard(w) for w in (w_gate, w_up, w_down.T)], axis=1)
    count, width = tokens.shape
    half = count // 2
    vm = pltpu.VMEM
    dma = pltpu.SemaphoreType.DMA
    scratch = [
        vm((ATT_CHUNKS, 4, NZ, 2, 2, ROWS, WIDE), BF16),
        vm((ff_chunks, 3, NZ, 2, 2, ROWS, WIDE), BF16),
        vm((half, width), BF16),
        vm((half, width), BF16),
        vm((ATT_CHUNKS, half, WIDE), BF16),
        vm((ATT_CHUNKS, half, WIDE), BF16),
        vm((ATT_CHUNKS, half, WIDE), BF16),
        vm((ATT_CHUNKS, half, WIDE), BF16),
        vm((ATT_CHUNKS, 4, 2, HALF, HALF), BF16),
        vm((half, width), F32),
        vm((count, width), BF16),
        vm((width, count), BF16),
        vm((count, width), BF16),
        vm((width, count), BF16),
        vm((half, width), F32),
        vm((half, width), F32),
        vm((2, WIDE, width), F32),
        vm((3, ff_chunks, count, WIDE), BF16),
        vm((half, width), BF16),
        vm((half, width), BF16),
        vm((2, 4, NZ, 2, ROWS, WIDE), BF16),
        vm((ff_chunks, 3, NZ, ROWS, WIDE), BF16),
        vm((ff_chunks, 3, 3, ROWS, WIDE), BF16),
        vm((ATT_CHUNKS, 4, NZ, ROWS, WIDE), BF16),
        vm((ATT_CHUNKS, 3, 4, ROWS, WIDE), BF16),
        vm((ATT_CHUNKS, 4, ROWS, HALF), BF16),
        vm((ATT_CHUNKS, 4, ROWS, HALF), F32),
        vm((ff_chunks, 3, ROWS, WIDE), F32),
        dma((2 + ATT_CHUNKS + ff_chunks,)),
        dma((ATT_CHUNKS, 10)),
        dma((ATT_CHUNKS, 10)),
        dma((ff_chunks, 6)),
        dma((ff_chunks, 6)),
        dma((ff_chunks, 5)),
        dma((ff_chunks, 5)),
        dma((ATT_CHUNKS, 6)),
        dma((ATT_CHUNKS, 6)),
        dma((8,)),
        dma((8,)),
        dma((ff_chunks + ATT_CHUNKS,)),
        pltpu.SemaphoreType.REGULAR,
    ]
    anywhere = pl.BlockSpec(memory_space=pl.ANY)
    block_out, grad_tokens, ga, gs = pl.pallas_call(
        functools.partial(layer_kernel, ff_chunks, ff_width),
        out_shape=(
            jax.ShapeDtypeStruct((count, width), BF16),
            jax.ShapeDtypeStruct((count, width), BF16),
            jax.ShapeDtypeStruct((ATT_CHUNKS, 4, ROWS, HALF), F32),
            jax.ShapeDtypeStruct((ff_chunks, 3, ROWS, WIDE), F32),
        ),
        in_specs=[anywhere] * 4,
        out_specs=(anywhere,) * 4,
        scratch_shapes=scratch,
        compiler_params=pltpu.CompilerParams(
            collective_id=0, has_side_effects=True, vmem_limit_bytes=67043328
        ),
        name="layer",
    )(tokens, out_grad, ash, ssh)

    def attention_grad(k):
        return ga[:, k].transpose(1, 0, 2).reshape(ROWS, ATT_CHUNKS * HALF)

    def gated_grad(k):
        return gs[:, k].transpose(1, 0, 2).reshape(ROWS, ff_chunks * WIDE)[:, :ff_width]

    return (
        block_out, grad_tokens, attention_grad(0), attention_grad(1), attention_grad(2),
        attention_grad(3).T, gated_grad(0), gated_grad(1), gated_grad(2).T,
    )


def fits(mesh, shapes):
    sizes = dict(mesh.shape)
    tokens, w_query, w_gate = shapes[0], shapes[1], shapes[5]
    return (
        sizes.get("dp") == 16
        and sizes.get("mp") == 2
        and tokens == (16384, 1024)
        and w_query == (1024, 1024)
        and w_gate[1] % (2 * HALF) == 0
        and 5 * WIDE < w_gate[1] // 2 <= 6 * WIDE
    )


def normalize(values_in):
    factor = lax.rsqrt(jnp.mean(values_in * values_in, axis=-1, keepdims=True) + eps)
    return (values_in * factor, factor)


def norm_back(grad_normed, normed, factor):
    return factor * (grad_normed - normed * jnp.mean(grad_normed * normed, axis=-1, keepdims=True))


def contract_rows(left, right):
    return lax.dot_general(
        left, right, (((0,), (0,)), ((), ())), preferred_element_type=jnp.float32
    )


def times_transposed(left, right):
    return lax.dot_general(
        left, right, (((1,), (1,)), ((), ())), preferred_element_type=jnp.float32
    )


def forward_product(left, right):
    return jnp.dot(left, right, preferred_element_type=jnp.float32)


def layer_pass(tokens_part, grad_part, weights):
    w_query, w_key, w_value, w_out, w_gate, w_up, w_down = weights
    count = tokens_part.shape[0]
    width = tokens_part.shape[1]
    head_dim = width // HEADS
    local = w_query.shape[1] // head_dim
    blocks = count // BLK
    scale = head_dim ** (-0.5)
    places = jnp.arange(BLK)
    causal = places[:, None] >= places[None, :]

    def split_heads(matrix):
        return matrix.reshape(blocks, BLK, local, head_dim).transpose(0, 2, 1, 3)

    def join_heads(stacked):
        return stacked.transpose(0, 2, 1, 3).reshape(count, local * head_dim)

    def scores_of(query, keys):
        raw = jnp.einsum("bhqd,bhkd->bhqk", query, keys, preferred_element_type=jnp.float32) * scale
        return jnp.where(causal, raw, -1e30)

    tokens_float = tokens_part.astype(jnp.float32)
    norm_one, factor_one = normalize(tokens_float)
    input_one = norm_one.astype(jnp.bfloat16)
    query = split_heads(forward_product(input_one, w_query).astype(jnp.bfloat16))
    keys = split_heads(forward_product(input_one, w_key).astype(jnp.bfloat16))
    values = split_heads(forward_product(input_one, w_value).astype(jnp.bfloat16))
    scores = scores_of(query, keys)
    peak = jnp.max(scores, axis=-1, keepdims=True)
    raised = jnp.exp(scores - peak)
    totals = jnp.sum(raised, axis=-1, keepdims=True)
    log_total = peak + jnp.log(totals)
    attend_low = (raised / totals).astype(jnp.bfloat16)
    mixed_heads = jnp.einsum(
        "bhqk,bhkd->bhqd", attend_low, values, preferred_element_type=jnp.float32
    )
    mixed = join_heads(mixed_heads.astype(jnp.bfloat16))
    branch_one = lax.psum(forward_product(mixed, w_out), "mp")
    resid = tokens_float + branch_one
    norm_two, factor_two = normalize(resid)
    input_two = norm_two.astype(jnp.bfloat16)
    gate = forward_product(input_two, w_gate)
    upper = forward_product(input_two, w_up)
    hidden = (gate * upper).astype(jnp.bfloat16)
    grad_down = contract_rows(hidden, grad_part)
    grad_hidden = times_transposed(grad_part, w_down)
    gate_back = (grad_hidden * upper).astype(jnp.bfloat16)
    up_back = (grad_hidden * gate).astype(jnp.bfloat16)
    grad_gate = contract_rows(input_two, gate_back)
    grad_up = contract_rows(input_two, up_back)
    two_partial = times_transposed(gate_back, w_gate) + times_transposed(up_back, w_up)
    branch_two = lax.psum(forward_product(hidden, w_down).astype(jnp.bfloat16), "mp").astype(
        jnp.float32
    )
    block_out = (resid + branch_two).astype(jnp.bfloat16)
    norm_two_back = lax.psum(two_partial, "mp")
    resid_back = grad_part.astype(jnp.float32) + norm_back(norm_two_back, norm_two, factor_two)
    branch_back = resid_back.astype(jnp.bfloat16)
    grad_out = contract_rows(mixed, branch_back)
    mixed_back = split_heads(times_transposed(branch_back, w_out).astype(jnp.bfloat16))
    attend = jnp.exp(scores_of(query, keys) - log_total)
    values_back = jnp.einsum(
        "bhqk,bhqd->bhkd", attend_low, mixed_back, preferred_element_type=jnp.float32
    )
    values_back = join_heads(values_back.astype(jnp.bfloat16))
    attend_back = jnp.einsum(
        "bhqd,bhkd->bhqk", mixed_back, values, preferred_element_type=jnp.float32
    )
    scores_back = attend * (attend_back - jnp.sum(attend_back * attend, axis=-1, keepdims=True))
    scores_back = scores_back.astype(jnp.bfloat16)
    query_back = scale * jnp.einsum(
        "bhqk,bhkd->bhqd", scores_back, keys, preferred_element_type=jnp.float32
    )
    query_back = join_heads(query_back.astype(jnp.bfloat16))
    keys_back = scale * jnp.einsum(
        "bhqk,bhqd->bhkd", scores_back, query, preferred_element_type=jnp.float32
    )
    keys_back = join_heads(keys_back.astype(jnp.bfloat16))
    grad_query = contract_rows(input_one, query_back)
    grad_key = contract_rows(input_one, keys_back)
    grad_value = contract_rows(input_one, values_back)
    one_partial = (
        times_transposed(query_back, w_query)
        + times_transposed(keys_back, w_key)
        + times_transposed(values_back, w_value)
    )
    norm_one_back = lax.psum(one_partial, "mp")
    grad_tokens = (resid_back + norm_back(norm_one_back, norm_one, factor_one)).astype(jnp.bfloat16)
    return (
        block_out,
        grad_tokens,
        (grad_query, grad_key, grad_value, grad_out, grad_gate, grad_up, grad_down),
    )


def body(tokens, w_query, w_key, w_value, w_out, w_gate, w_up, w_down, out_grad):
    count = tokens.shape[0] // MICRO
    outputs = []
    backs = []
    summed = None
    for number in range(MICRO):
        weights = (
            lax.all_gather(w_query, "dp", axis=0, tiled=True),
            lax.all_gather(w_key, "dp", axis=0, tiled=True),
            lax.all_gather(w_value, "dp", axis=0, tiled=True),
            lax.all_gather(w_out, "dp", axis=1, tiled=True),
            lax.all_gather(w_gate, "dp", axis=0, tiled=True),
            lax.all_gather(w_up, "dp", axis=0, tiled=True),
            lax.all_gather(w_down, "dp", axis=1, tiled=True),
        )
        first = number * count
        block_out, grad_tokens, grads = layer_pass(
            tokens[first : first + count], out_grad[first : first + count], weights
        )
        outputs.append(block_out)
        backs.append(grad_tokens)
        if number == 0:
            summed = tuple(grads)
        else:
            summed = tuple(jax.tree.map(jnp.add, tuple(summed), tuple(grads)))
    summed = (
        lax.psum_scatter(summed[0], "dp", scatter_dimension=0, tiled=True),
        lax.psum_scatter(summed[1], "dp", scatter_dimension=0, tiled=True),
        lax.psum_scatter(summed[2], "dp", scatter_dimension=0, tiled=True),
        lax.psum_scatter(summed[3], "dp", scatter_dimension=1, tiled=True),
        lax.psum_scatter(summed[4], "dp", scatter_dimension=0, tiled=True),
        lax.psum_scatter(summed[5], "dp", scatter_dimension=0, tiled=True),
        lax.psum_scatter(summed[6], "dp", scatter_dimension=1, tiled=True),
    )
    return (
        jnp.concatenate(outputs, axis=0),
        jnp.concatenate(backs, axis=0),
        summed[0],
        summed[1],
        summed[2],
        summed[3],
        summed[4],
        summed[5],
        summed[6],
    )


def solution(mesh):
    in_specs = (
        P("dp", None),
        P("dp", "mp"),
        P("dp", "mp"),
        P("dp", "mp"),
        P("mp", "dp"),
        P("dp", "mp"),
        P("dp", "mp"),
        P("mp", "dp"),
        P("dp", None),
    )
    out_specs = (
        P("dp", None),
        P("dp", None),
        P("dp", "mp"),
        P("dp", "mp"),
        P("dp", "mp"),
        P("mp", "dp"),
        P("dp", "mp"),
        P("dp", "mp"),
        P("mp", "dp"),
    )

    def program(*args):
        shapes = [a.shape for a in args]
        if fits(mesh, shapes):
            ff_width = shapes[5][1] // 2
            chosen = functools.partial(fast_body, pl.cdiv(ff_width, WIDE), ff_width)
        else:
            chosen = body
        return jax.shard_map(
            chosen, mesh=mesh, in_specs=in_specs, out_specs=out_specs, check_vma=False
        )(*args)

    return program
```
